32 devices in a mesh: tm: 2 (over core), station: 4 (over y, x), channel: 4 (over z).
Axes of the slice: x: 2, y: 2, z: 4, core: 2. Of those that a mesh axis runs over, the one named last changes fastest.
Arguments:
- voltages: bfloat16 [2, 32, 2, 512, 512], P(None, 'channel', None, 'station', 'tm'), may hold values from -64 to 64
- start_seed: int32 [2, 32, 4, 2, 512], P(None, 'channel', None, None, 'station'), may hold values from -8 to 8
- beam_phase: int32 [512, 512], replicated, may hold values from 0 to 1023
- station_delay: int32 [512], replicated, may hold values from 0 to 1023
Outputs:
- beam_output: bfloat16 [2, 32, 2, 512, 512], P(None, 'channel', None, 'station', 'tm')
- subspace: float32 [2, 32, 4, 2, 512], P(None, 'channel', None, None, 'station')
The draws below stay inside these ranges and needn't reach their ends.
All inputs are finite; a program needn't handle non-finite values.
Results may differ from the reference program's by a relative error of at most 0.017.
Values may be sent and summed in bfloat16 or wider, within the bound.
No kernel may reach another device: no remote copies, remote signals or barrier semaphores. Data moves between devices by JAX's collectives and lax.ppermute only.
A program may use at most 64 MiB of HBM per device.

```python
import jax
import jax.numpy as jnp
from jax import lax

STATIONS = 512
POLS = 2
CHANNELS = 32
BEAMS = 512
RANK = 4
ITERS = 3
PHASES = 1024
TIME = 512


def draw_voltages(key, part):
    subkeys = jax.random.split(jax.random.fold_in(key, 11), 5)
    full_shape = (2, CHANNELS, POLS, STATIONS, TIME)
    thermal = jax.random.normal(subkeys[0], full_shape, jnp.float32)
    strength = jnp.exp(jax.random.uniform(subkeys[1], (CHANNELS, RANK), jnp.float32, jnp.log(4.0), jnp.log(80.0)))
    amplitude = jnp.exp(jax.random.uniform(subkeys[2], (CHANNELS,), jnp.float32, 0.0, jnp.log(3.3)))
    steering = jax.random.normal(subkeys[3], (2, CHANNELS, RANK, POLS, STATIONS), jnp.float32) * jnp.sqrt(0.5)
    signal = jax.random.normal(subkeys[4], (2, CHANNELS, RANK, TIME), jnp.float32) * jnp.sqrt(0.5)
    strength_root = jnp.sqrt(strength / (POLS * STATIONS))
    signal = signal * strength_root[None, :, :, None]
    pattern = 'ckpm,ckt->cpmt'
    real_sum = jnp.einsum(pattern, steering[0], signal[0]) - jnp.einsum(pattern, steering[1], signal[1])
    imag_sum = jnp.einsum(pattern, steering[0], signal[1]) + jnp.einsum(pattern, steering[1], signal[0])
    growth = jnp.exp(jnp.log(3.0) * jnp.arange(TIME, dtype=jnp.float32) / TIME)
    envelope = amplitude[:, None, None, None] * growth[None, None, None, :]
    voltage = (thermal + jnp.stack([real_sum, imag_sum])) * envelope[None]
    return jnp.clip(voltage, -64.0, 64.0).astype(jnp.bfloat16)


def set_ends(array, stream_key, low, high):
    extent = array.shape
    index_at = [jax.random.randint(jax.random.fold_in(stream_key, axis), (), 0, extent[axis]) for axis in range(len(extent))]
    array = array.at[tuple(index_at)].set(low)
    longest = extent.index(max(extent))
    index_at[longest] = (index_at[longest] + 1) % extent[longest]
    return array.at[tuple(index_at)].set(high)


def setup_inputs(seed: int = 0) -> dict:
    key_of = jax.random.split(jax.random.key(seed), 5)
    return {
        "voltages": draw_voltages(jax.random.fold_in(key_of[4], 71), 0),
        "start_seed": set_ends(jax.random.randint(key_of[1], (2, CHANNELS, RANK, POLS, STATIONS), -8, 9), jax.random.fold_in(key_of[1], 1), -8, 8).astype(jnp.int32),
        "beam_phase": set_ends(jax.random.randint(key_of[2], (BEAMS, STATIONS), 0, PHASES), jax.random.fold_in(key_of[2], 1), 0, PHASES - 1).astype(jnp.int32),
        "station_delay": set_ends(jax.random.randint(key_of[3], (STATIONS,), 0, PHASES), jax.random.fold_in(key_of[3], 1), 0, PHASES - 1).astype(jnp.int32),
    }


HIGH = lax.Precision.HIGHEST

def coefficients(subspace, voltage):
    real_v = voltage[0].astype(jnp.float32)
    imag_v = voltage[1].astype(jnp.float32)
    pattern = '...kpm,...pmt->...kt'
    real_sum = jnp.einsum(pattern, subspace[0], real_v, precision=HIGH) + jnp.einsum(pattern, subspace[1], imag_v, precision=HIGH)
    imag_sum = jnp.einsum(pattern, subspace[0], imag_v, precision=HIGH) - jnp.einsum(pattern, subspace[1], real_v, precision=HIGH)
    return jnp.stack([real_sum, imag_sum])

def applied(voltage, coefficient):
    real_v = voltage[0].astype(jnp.float32)
    imag_v = voltage[1].astype(jnp.float32)
    pattern = '...pmt,...kt->...kpm'
    real_sum = jnp.einsum(pattern, real_v, coefficient[0], precision=HIGH) + jnp.einsum(pattern, imag_v, coefficient[1], precision=HIGH)
    imag_sum = jnp.einsum(pattern, imag_v, coefficient[0], precision=HIGH) - jnp.einsum(pattern, real_v, coefficient[1], precision=HIGH)
    return jnp.stack([real_sum, imag_sum])

def gram_matrix(image_field):
    pattern = '...kpm,...lpm->...kl'
    real_sum = jnp.einsum(pattern, image_field[0], image_field[0], precision=HIGH) + jnp.einsum(pattern, image_field[1], image_field[1], precision=HIGH)
    imag_sum = jnp.einsum(pattern, image_field[0], image_field[1], precision=HIGH) - jnp.einsum(pattern, image_field[1], image_field[0], precision=HIGH)
    return jnp.stack([real_sum, imag_sum])

def inverse_factor(gram_real, gram_imag):
    rank_count = gram_real.shape[-1]
    nothing = jnp.zeros_like(gram_real[..., 0, 0])
    low_real = {}
    low_imag = {}
    for column in range(rank_count):
        diagonal = gram_real[..., column, column]
        for middle in range(column):
            diagonal = diagonal - low_real[column, middle] ** 2 - low_imag[column, middle] ** 2
        pivot_root = jnp.sqrt(diagonal)
        low_real[column, column] = pivot_root
        low_imag[column, column] = nothing
        for row_at in range(column + 1, rank_count):
            acc_real = gram_real[..., row_at, column]
            acc_imag = gram_imag[..., row_at, column]
            for middle in range(column):
                acc_real = acc_real - (low_real[row_at, middle] * low_real[column, middle] + low_imag[row_at, middle] * low_imag[column, middle])
                acc_imag = acc_imag - (low_imag[row_at, middle] * low_real[column, middle] - low_real[row_at, middle] * low_imag[column, middle])
            low_real[row_at, column] = acc_real / pivot_root
            low_imag[row_at, column] = acc_imag / pivot_root
    inv_real = {}
    inv_imag = {}
    for column in range(rank_count):
        inv_real[column, column] = 1.0 / low_real[column, column]
        inv_imag[column, column] = nothing
        for row_at in range(column + 1, rank_count):
            acc_real = nothing
            acc_imag = nothing
            for middle in range(column, row_at):
                acc_real = acc_real + low_real[row_at, middle] * inv_real[middle, column] - low_imag[row_at, middle] * inv_imag[middle, column]
                acc_imag = acc_imag + low_real[row_at, middle] * inv_imag[middle, column] + low_imag[row_at, middle] * inv_real[middle, column]
            inv_real[row_at, column] = -acc_real / low_real[row_at, row_at]
            inv_imag[row_at, column] = -acc_imag / low_real[row_at, row_at]
    real_rows = [jnp.stack([inv_real.get((row_at, column), nothing) for column in range(rank_count)], axis=-1) for row_at in range(rank_count)]
    imag_rows = [jnp.stack([inv_imag.get((row_at, column), nothing) for column in range(rank_count)], axis=-1) for row_at in range(rank_count)]
    return (jnp.stack(real_rows, axis=-2), jnp.stack(imag_rows, axis=-2))

def orthonormal(image_field, sums):
    inv_real, inv_imag = inverse_factor(sums[0], sums[1])
    pattern = '...lpm,...kl->...kpm'
    real_sum = jnp.einsum(pattern, image_field[0], inv_real, precision=HIGH) + jnp.einsum(pattern, image_field[1], inv_imag, precision=HIGH)
    imag_sum = jnp.einsum(pattern, image_field[1], inv_real, precision=HIGH) - jnp.einsum(pattern, image_field[0], inv_imag, precision=HIGH)
    return jnp.stack([real_sum, imag_sum])

def project_out(voltage, subspace, coefficient):
    pattern = '...kpm,...kt->...pmt'
    real_sum = jnp.einsum(pattern, subspace[0], coefficient[0], precision=HIGH) - jnp.einsum(pattern, subspace[1], coefficient[1], precision=HIGH)
    imag_sum = jnp.einsum(pattern, subspace[0], coefficient[1], precision=HIGH) + jnp.einsum(pattern, subspace[1], coefficient[0], precision=HIGH)
    return jnp.stack([voltage[0].astype(jnp.float32) - real_sum, voltage[1].astype(jnp.float32) - imag_sum])

def beam_weights(phase_rows, delays, channel_numbers):
    summed = phase_rows + delays[None, :]
    index = summed[None, :, :] * (channel_numbers[:, None, None] + 1) % PHASES
    angle = index.astype(jnp.float32) * (2.0 * jnp.pi / PHASES)
    norming = 1.0 / jnp.sqrt(jnp.float32(STATIONS))
    return ((jnp.cos(angle) * norming).astype(jnp.bfloat16), (-jnp.sin(angle) * norming).astype(jnp.bfloat16))

def form_beams(real_w, imag_w, cleaned):
    pattern = '...bm,...pmt->...pbt'
    real_w = real_w.astype(jnp.float32)
    imag_w = imag_w.astype(jnp.float32)
    real_c = cleaned[0].astype(jnp.float32)
    imag_c = cleaned[1].astype(jnp.float32)
    real_sum = jnp.einsum(pattern, real_w, real_c, precision=HIGH) - jnp.einsum(pattern, imag_w, imag_c, precision=HIGH)
    imag_sum = jnp.einsum(pattern, real_w, imag_c, precision=HIGH) + jnp.einsum(pattern, imag_w, real_c, precision=HIGH)
    return jnp.stack([real_sum, imag_sum])

def reference(voltages, start_seed, beam_phase, station_delay):

    def per_channel(inputs):
        voltage, start_field, channel_number = inputs
        subspace = start_field.astype(jnp.float32)
        for iteration in range(ITERS):
            summed = applied(voltage, coefficients(subspace, voltage))
            subspace = orthonormal(summed, gram_matrix(summed))
        cleaned = project_out(voltage, subspace, coefficients(subspace, voltage)).astype(jnp.bfloat16)
        real_w, imag_w = beam_weights(beam_phase, station_delay, channel_number.reshape(1))
        beam_field = form_beams(real_w[0], imag_w[0], cleaned)
        return (subspace, beam_field)
    numbers = jnp.arange(CHANNELS, dtype=jnp.int32)
    subspace_all, beams_all = lax.map(per_channel, (jnp.moveaxis(voltages, 1, 0), jnp.moveaxis(start_seed, 1, 0), numbers))
    beam_power = lax.optimization_barrier(jnp.sum(beams_all[:, 0] ** 2 + beams_all[:, 1] ** 2, axis=(0, 3))) / (CHANNELS * TIME)
    rescale = lax.rsqrt(beam_power + 1e-06)
    beam_output = (beams_all * rescale[None, None, :, :, None]).astype(jnp.bfloat16)
    return (jnp.moveaxis(beam_output, 0, 1), jnp.moveaxis(subspace_all, 0, 1))
```

```python
import functools

import jax
import jax.numpy as jnp
from jax import lax
from jax.experimental import pallas as pl
from jax.experimental.pallas import tpu as pltpu
from jax.sharding import PartitionSpec as P

ITERS = 3
PHASES = 1024
GROUP = ("tm", "station")


HIGH = lax.Precision.HIGHEST
VMEM = pltpu.MemorySpace.VMEM
SMEM = pltpu.MemorySpace.SMEM
HBM = pltpu.MemorySpace.HBM


def coefficients(subspace, voltage):
    real_v = voltage[0].astype(jnp.float32)
    imag_v = voltage[1].astype(jnp.float32)
    pattern = "...kpm,...pmt->...kt"
    real_sum = jnp.einsum(pattern, subspace[0], real_v, precision=HIGH) + jnp.einsum(
        pattern, subspace[1], imag_v, precision=HIGH
    )
    imag_sum = jnp.einsum(pattern, subspace[0], imag_v, precision=HIGH) - jnp.einsum(
        pattern, subspace[1], real_v, precision=HIGH
    )
    return jnp.stack([real_sum, imag_sum])


def applied(voltage, coefficient):
    real_v = voltage[0].astype(jnp.float32)
    imag_v = voltage[1].astype(jnp.float32)
    pattern = "...pmt,...kt->...kpm"
    real_sum = jnp.einsum(pattern, real_v, coefficient[0], precision=HIGH) + jnp.einsum(
        pattern, imag_v, coefficient[1], precision=HIGH
    )
    imag_sum = jnp.einsum(pattern, imag_v, coefficient[0], precision=HIGH) - jnp.einsum(
        pattern, real_v, coefficient[1], precision=HIGH
    )
    return jnp.stack([real_sum, imag_sum])


def gram_matrix(image_field):
    pattern = "...kpm,...lpm->...kl"
    real_sum = jnp.einsum(pattern, image_field[0], image_field[0], precision=HIGH) + jnp.einsum(
        pattern, image_field[1], image_field[1], precision=HIGH
    )
    imag_sum = jnp.einsum(pattern, image_field[0], image_field[1], precision=HIGH) - jnp.einsum(
        pattern, image_field[1], image_field[0], precision=HIGH
    )
    return jnp.stack([real_sum, imag_sum])


def inverse_factor(gram_real, gram_imag):
    rank_count = gram_real.shape[-1]
    nothing = jnp.zeros_like(gram_real[..., 0, 0])
    low_real = {}
    low_imag = {}
    for column in range(rank_count):
        diagonal = gram_real[..., column, column]
        for middle in range(column):
            diagonal = diagonal - low_real[column, middle] ** 2 - low_imag[column, middle] ** 2
        pivot_root = jnp.sqrt(diagonal)
        low_real[column, column] = pivot_root
        low_imag[column, column] = nothing
        for row_at in range(column + 1, rank_count):
            acc_real = gram_real[..., row_at, column]
            acc_imag = gram_imag[..., row_at, column]
            for middle in range(column):
                acc_real = acc_real - (
                    low_real[row_at, middle] * low_real[column, middle]
                    + low_imag[row_at, middle] * low_imag[column, middle]
                )
                acc_imag = acc_imag - (
                    low_imag[row_at, middle] * low_real[column, middle]
                    - low_real[row_at, middle] * low_imag[column, middle]
                )
            low_real[row_at, column] = acc_real / pivot_root
            low_imag[row_at, column] = acc_imag / pivot_root
    inv_real = {}
    inv_imag = {}
    for column in range(rank_count):
        inv_real[column, column] = 1.0 / low_real[column, column]
        inv_imag[column, column] = nothing
        for row_at in range(column + 1, rank_count):
            acc_real = nothing
            acc_imag = nothing
            for middle in range(column, row_at):
                acc_real = (
                    acc_real
                    + low_real[row_at, middle] * inv_real[middle, column]
                    - low_imag[row_at, middle] * inv_imag[middle, column]
                )
                acc_imag = (
                    acc_imag
                    + low_real[row_at, middle] * inv_imag[middle, column]
                    + low_imag[row_at, middle] * inv_real[middle, column]
                )
            inv_real[row_at, column] = -acc_real / low_real[row_at, row_at]
            inv_imag[row_at, column] = -acc_imag / low_real[row_at, row_at]
    span = range(rank_count)
    real_rows = [jnp.stack([inv_real.get((r, c), nothing) for c in span], axis=-1) for r in span]
    imag_rows = [jnp.stack([inv_imag.get((r, c), nothing) for c in span], axis=-1) for r in span]
    return (jnp.stack(real_rows, axis=-2), jnp.stack(imag_rows, axis=-2))


def orthonormal(image_field, sums):
    inv_real, inv_imag = inverse_factor(sums[0], sums[1])
    pattern = "...lpm,...kl->...kpm"
    real_sum = jnp.einsum(pattern, image_field[0], inv_real, precision=HIGH) + jnp.einsum(
        pattern, image_field[1], inv_imag, precision=HIGH
    )
    imag_sum = jnp.einsum(pattern, image_field[1], inv_real, precision=HIGH) - jnp.einsum(
        pattern, image_field[0], inv_imag, precision=HIGH
    )
    return jnp.stack([real_sum, imag_sum])


def project_out(voltage, subspace, coefficient):
    pattern = "...kpm,...kt->...pmt"
    real_sum = jnp.einsum(pattern, subspace[0], coefficient[0], precision=HIGH) - jnp.einsum(
        pattern, subspace[1], coefficient[1], precision=HIGH
    )
    imag_sum = jnp.einsum(pattern, subspace[0], coefficient[1], precision=HIGH) + jnp.einsum(
        pattern, subspace[1], coefficient[0], precision=HIGH
    )
    return jnp.stack(
        [voltage[0].astype(jnp.float32) - real_sum, voltage[1].astype(jnp.float32) - imag_sum]
    )


def beam_weights(phase_rows, delays, channel_numbers):
    summed = phase_rows + delays[None, :]
    index = summed[None, :, :] * (channel_numbers[:, None, None] + 1) % PHASES
    angle = index.astype(jnp.float32) * (2.0 * jnp.pi / PHASES)
    norming = 1.0 / jnp.sqrt(jnp.float32(delays.shape[0]))
    return (
        (jnp.cos(angle) * norming).astype(jnp.bfloat16),
        (-jnp.sin(angle) * norming).astype(jnp.bfloat16),
    )


def form_beams(real_w, imag_w, cleaned):
    dot = functools.partial(jnp.einsum, "cbm,cpmt->cpbt", preferred_element_type=jnp.float32)
    real_sum = dot(real_w, cleaned[0]) - dot(imag_w, cleaned[1])
    imag_sum = dot(real_w, cleaned[1]) + dot(imag_w, cleaned[0])
    return jnp.stack([real_sum, imag_sum])


def general_body(voltages, start_seed, beam_phase, station_delay):
    chan_count = voltages.shape[1]
    first_channel = lax.axis_index("channel") * chan_count
    channel_numbers = jnp.arange(chan_count, dtype=jnp.int32) + first_channel
    subspace = start_seed.astype(jnp.float32)
    for iteration in range(ITERS):
        coefficient = lax.psum(
            coefficients(subspace, voltages).astype(jnp.bfloat16), "station"
        ).astype(jnp.float32)
        summed = lax.psum(applied(voltages, coefficient), "tm")
        sums = lax.psum(gram_matrix(summed), "station")
        subspace = orthonormal(summed, sums)
    coefficient = lax.psum(coefficients(subspace, voltages).astype(jnp.bfloat16), "station").astype(
        jnp.float32
    )
    cleaned = project_out(voltages, subspace, coefficient).astype(jnp.bfloat16)
    beam_count = beam_phase.shape[0] // lax.axis_size("station")
    first_beam = lax.axis_index("station") * beam_count
    phase_rows = lax.dynamic_slice_in_dim(beam_phase, first_beam, beam_count, 0)
    real_w, imag_w = beam_weights(phase_rows, station_delay, channel_numbers)
    beam_field = form_beams(real_w, imag_w, lax.all_gather(cleaned, "station", axis=3, tiled=True))
    power_part = jnp.sum(beam_field[0] ** 2 + beam_field[1] ** 2, axis=(0, 3))
    terms = chan_count * lax.axis_size("channel") * voltages.shape[4] * lax.axis_size("tm")
    beam_power = lax.psum(power_part, ("tm", "channel")) / terms
    rescale = lax.rsqrt(beam_power + 1e-06)
    beam_output = (beam_field * rescale[None, None, :, :, None]).astype(jnp.bfloat16)
    return (beam_output, subspace)


def pack_kernel(me_ref, volt_ref, seed_ref, *refs):
    group = len(refs) - 1
    outs, sem = refs[:group], refs[group]
    me = me_ref[0]
    rows = volt_ref.shape[2]
    copies = []
    for place in range(group):
        for part in range(2):
            copy = pltpu.make_async_copy(
                volt_ref.at[part, me ^ place],
                outs[place].at[pl.ds(part * rows, rows)],
                sem.at[place, part],
            )
            copy.start()
            copies.append(copy)
    rank = seed_ref.shape[2] // 2
    for place in range(group):
        halves = []
        for part in range(2):
            pols = [
                seed_ref[part, me ^ place, pl.ds(pol, rank, stride=2), :] for pol in range(2)
            ]
            halves.append(jnp.concatenate(pols, axis=1))
        start = jnp.concatenate(halves, axis=0).astype(jnp.float32)
        start = jnp.concatenate([start, jnp.zeros_like(start)], axis=0)
        outs[place][2 * rows :, :] = start.astype(jnp.bfloat16)
    for copy in copies:
        copy.wait()


def cos_sin(index):
    quarter = PHASES // 4
    turn = (index + quarter // 2) // quarter if quarter & (quarter - 1) else (
        (index + quarter // 2) >> (quarter.bit_length() - 1)
    )
    rest = index - turn * quarter
    angle = rest.astype(jnp.float32) * (2.0 * jnp.pi / PHASES)
    square = angle * angle
    cos = 1.0 + square * (
        -0.5 + square * (1.0 / 24 + square * (-1.0 / 720 + square * (1.0 / 40320)))
    )
    sin = angle * (
        1.0 + square * (-1.0 / 6 + square * (1.0 / 120 + square * (-1.0 / 5040 + square * (1.0 / 362880))))
    )
    odd = (turn & 1) == 1
    base_cos = jnp.where(odd, sin, cos)
    base_sin = jnp.where(odd, cos, sin)
    flip_cos = ((turn + 1) & 2) == 2
    flip_sin = (turn & 2) == 2
    return jnp.where(flip_cos, -base_cos, base_cos), jnp.where(flip_sin, -base_sin, base_sin)


def weight_kernel(stations, scalars_ref, phase_ref, delay_ref, out_ref):
    mine, number = scalars_ref[0], scalars_ref[1]
    beams = phase_ref.shape[0]
    wide = stations
    places = phase_ref.shape[1] // wide
    norming = 1.0 / jnp.sqrt(jnp.float32(phase_ref.shape[1]))
    for place in range(places):
        column = pl.multiple_of((mine ^ place) * wide, wide)
        summed = phase_ref[:, pl.ds(column, wide)] + delay_ref[:, pl.ds(column, wide)]
        cos, sin = cos_sin((summed * number) & (PHASES - 1))
        real = (cos * norming).astype(jnp.bfloat16)
        imag = (-sin * norming).astype(jnp.bfloat16)
        first = pl.ds(place * wide, wide)
        second = pl.ds((places + place) * wide, wide)
        out_ref[:beams, first] = real
        out_ref[:beams, second] = -imag
        out_ref[beams:, first] = imag
        out_ref[beams:, second] = real


def split(value, count):
    parts = []
    for _ in range(count - 1):
        part = value.astype(jnp.bfloat16)
        parts.append(part)
        value = value - part.astype(jnp.float32)
    return parts + [value.astype(jnp.bfloat16)]


def nn(a, b):
    return lax.dot_general(a, b, (((1,), (0,)), ((), ())), preferred_element_type=jnp.float32)


def nt(a, b):
    return lax.dot_general(a, b, (((1,), (1,)), ((), ())), preferred_element_type=jnp.float32)


def tn(a, b):
    return lax.dot_general(a, b, (((0,), (0,)), ((), ())), preferred_element_type=jnp.float32)


def middle_kernel(places, halves, rank, pols, *refs):
    group = places * halves
    x = refs[:group]
    weight_ref = refs[group]
    y = refs[group + 1 : 2 * group + 1]
    power_ref = refs[2 * group + 1]
    clean_ref, sum_ref = refs[2 * group + 2 :]
    inputs = (x[0].shape[0] - 4 * rank) // 2
    wide = inputs // pols
    times = x[0].shape[1]
    rows = 2 * rank
    row_at = lax.broadcasted_iota(jnp.int32, (rows, 1), 0)
    top = row_at < rank
    sign = jnp.where(top, 1.0, -1.0).astype(jnp.float32)
    row_mod = jnp.where(top, row_at, row_at - rank)

    def swap(value):
        return jnp.concatenate([value[rank:], value[:rank]], axis=0)

    def fold(value):
        total = value[:rows]
        for piece in range(1, value.shape[0] // rows):
            total = total + value[piece * rows : (piece + 1) * rows]
        return total

    def coefficient_of(field, count):
        left = []
        for value in field:
            both = jnp.concatenate([sign * value, swap(value)], axis=1)
            left.append(jnp.concatenate(split(both, count), axis=0))
        out = []
        for half in range(halves):
            total = None
            for place in range(places):
                term = nn(left[place], x[half * places + place][: 2 * inputs, :])
                total = term if total is None else total + term
            out.append(fold(total))
        return out

    def image_of(coefficient):
        left = [jnp.concatenate(split(value, 3), axis=0) for value in coefficient]
        out = []
        for place in range(places):
            total = None
            for half in range(halves):
                term = nt(left[half], x[half * places + place][: 2 * inputs, :])
                total = term if total is None else total + term
            total = fold(total)
            out.append(swap(total[:, inputs:]) + sign * total[:, :inputs])
        return out

    def whitener(field):
        column = []
        for line in range(rows):
            total = None
            for value in field:
                term = jnp.sum(value * value[line : line + 1], axis=1, keepdims=True)
                total = term if total is None else total + term
            column.append(total)
        real, imag = [], []
        for line in range(rank):
            value = column[line] + swap(column[line + rank])
            real.append(jnp.where(top, value, swap(value)))
            value = column[line + rank] - swap(column[line])
            imag.append(jnp.where(top, value, swap(value)))
        zero = jnp.zeros((rows, 1), jnp.float32)
        inv_real = [jnp.where(row_mod == line, 1.0, zero) for line in range(rank)]
        inv_imag = [zero] * rank
        pivots = zero
        for step in range(rank):
            pivot = real[step][step : step + 1]
            pivots = jnp.where(row_mod == step, pivot, pivots)
            if step == rank - 1:
                break
            below = row_mod > step
            inverse = 1.0 / pivot
            mul_real = jnp.where(below, real[step] * inverse, 0.0)
            mul_imag = jnp.where(below, imag[step] * inverse, 0.0)

            def reduce(re, im):
                at_re, at_im = re[step : step + 1], im[step : step + 1]
                return (
                    re - (mul_real * at_re - mul_imag * at_im),
                    im - (mul_real * at_im + mul_imag * at_re),
                )

            for line in range(step + 1, rank):
                real[line], imag[line] = reduce(real[line], imag[line])
            for line in range(step + 1):
                inv_real[line], inv_imag[line] = reduce(inv_real[line], inv_imag[line])
        scale = 1.0 / jnp.sqrt(pivots)
        return [value * scale for value in inv_real], [value * scale for value in inv_imag]

    def basis(field, white):
        real, imag = white
        out = []
        for value in field:
            total = jnp.zeros_like(value)
            for line in range(rank):
                total = total + jnp.where(top, real[line], -imag[line]) * value[line : line + 1]
                total = total + jnp.where(top, imag[line], real[line]) * value[line + rank : line + rank + 1]
            out.append(total)
        return out

    def whitened(raw, white):
        real, imag = white
        out = []
        for value in raw:
            total = jnp.zeros_like(value)
            for line in range(rank):
                total = total + jnp.where(top, real[line], imag[line]) * value[line : line + 1]
                total = total + jnp.where(top, -imag[line], real[line]) * value[line + rank : line + rank + 1]
            out.append(total)
        return out

    start = [x[place][2 * inputs : 2 * inputs + rows, :].astype(jnp.float32) for place in range(places)]
    coefficient = coefficient_of(start, 1)
    for iteration in range(ITERS):
        field = image_of(coefficient)
        raw = coefficient_of(field, 3)
        white = whitener(field)
        coefficient = whitened(raw, white)
    subspace = basis(field, white)

    right = []
    for value in coefficient:
        both = jnp.concatenate([sign * value, swap(value)], axis=1)
        high, low = split(both, 2)
        right.append(jnp.concatenate([high, high, low], axis=0))
    for place in range(places):
        high, low = split(subspace[place], 2)
        for half in range(halves):
            y[half * places + place][2 * inputs :, :] = jnp.concatenate([high, low], axis=0)
        left = jnp.concatenate([high, low, high], axis=0)
        for half in range(halves):
            gone = tn(left, right[half])
            for part in range(2):
                for pol in range(pols):
                    at = part * inputs + pol * wide
                    value = x[half * places + place][at : at + wide, :].astype(jnp.float32)
                    value = value - gone[pol * wide : (pol + 1) * wide, part * times : (part + 1) * times]
                    first = (part * places + place) * wide
                    clean_ref[pol, half, first : first + wide, :] = value.astype(jnp.bfloat16)

    beams = weight_ref.shape[0] // (2 * places)
    for half in range(halves):
        for pol in range(pols):
            for place in range(places):
                out = nn(
                    weight_ref[2 * place * beams : 2 * (place + 1) * beams, :], clean_ref[pol, half]
                )
                for part in range(2):
                    at = part * inputs + pol * beams
                    y[half * places + place][at : at + beams, :] = out[
                        part * beams : (part + 1) * beams
                    ].astype(jnp.bfloat16)
                square = out * out
                square = square[:beams] + square[beams:]
                lanes = square[:, :128]
                for lane in range(128, times, 128):
                    lanes = lanes + square[:, lane : lane + 128]
                if half == 0:
                    sum_ref[place * pols + pol] = lanes
                else:
                    sum_ref[place * pols + pol] += lanes
    for line in range(places * pols):
        power_ref[line : line + 1, :] = jnp.sum(sum_ref[line].T, axis=0, keepdims=True)


def finish_kernel(terms, me_ref, power_ref, *refs):
    group = (len(refs) - 4) if False else None
    del group
    *y, out_ref, base_ref, held, sem = refs
    me = me_ref[0]
    pols = power_ref.shape[0]
    beams = power_ref.shape[1]
    rescale = lax.rsqrt(power_ref[...] * (1.0 / terms) + 1e-06)
    square = jnp.concatenate([rescale, jnp.zeros((beams - pols, beams), jnp.float32)], axis=0).T
    scale = [jnp.broadcast_to(square[:, pol : pol + 1], (beams, y[0].shape[1])) for pol in range(pols)]
    inputs = pols * beams
    copies = []
    for place, source in enumerate(y):
        for part in range(2):
            for pol in range(pols):
                at = part * inputs + pol * beams
                value = source[at : at + beams, :].astype(jnp.float32) * scale[pol]
                held[place, part, pol * beams : (pol + 1) * beams, :] = value.astype(jnp.bfloat16)
            copy = pltpu.make_async_copy(
                held.at[place, part], out_ref.at[part, me ^ place], sem.at[place, part]
            )
            copy.start()
            copies.append(copy)
    rows = (y[0].shape[0] - 2 * inputs) // 2
    rank = rows // 2
    for place, source in enumerate(y):
        both = source[2 * inputs :, :].astype(jnp.float32)
        value = both[:rows] + both[rows:]
        for part in range(2):
            for pol in range(pols):
                base_ref[part, me ^ place, pl.ds(pol, rank, stride=pols), :] = value[
                    part * rank : (part + 1) * rank, pol * beams : (pol + 1) * beams
                ]
    for copy in copies:
        copy.wait()


def fast_body(voltages, start_seed, beam_phase, station_delay):
    parts, chan_count, pols, stations, times = voltages.shape
    rank = start_seed.shape[2]
    places, halves = lax.axis_size("station"), lax.axis_size("tm")
    group = places * halves
    inputs = pols * stations
    station_at, tm_at = lax.axis_index("station"), lax.axis_index("tm")
    me = (tm_at * places + station_at).astype(jnp.int32)
    number = (lax.axis_index("channel") * chan_count + me + 1).astype(jnp.int32)
    me_array = me.reshape(1)
    rows = 2 * inputs + 4 * rank
    block = jax.ShapeDtypeStruct((rows, times), jnp.bfloat16)
    vmem = pl.BlockSpec(memory_space=VMEM)
    smem = pl.BlockSpec(memory_space=SMEM)
    hbm = pl.BlockSpec(memory_space=HBM)

    def swap_with(value, offset):
        pairs = [(at, at ^ offset) for at in range(group)]
        return lax.ppermute(value, GROUP, pairs)

    packed = pl.pallas_call(
        pack_kernel,
        out_shape=[block] * group,
        in_specs=[smem, hbm, vmem],
        out_specs=[vmem] * group,
        scratch_shapes=[pltpu.SemaphoreType.DMA((group, 2))],
        cost_estimate=pl.CostEstimate(
            flops=0, transcendentals=0, bytes_accessed=4 * group * rows * times
        ),
    )(
        me_array,
        voltages.reshape(2, chan_count, inputs, times),
        start_seed.reshape(2, chan_count, rank * pols, stations),
    )
    held = [packed[0]] + [swap_with(packed[o], o) for o in range(1, group)]

    total_stations = places * stations
    beams = beam_phase.shape[0] // places
    weights = pl.pallas_call(
        functools.partial(weight_kernel, stations),
        out_shape=jax.ShapeDtypeStruct((2 * places * beams, 2 * total_stations), jnp.bfloat16),
        grid_spec=pltpu.PrefetchScalarGridSpec(
            num_scalar_prefetch=1,
            grid=(places,),
            in_specs=[
                pl.BlockSpec((beams, total_stations), lambda at, ref: (ref[0] ^ at, 0)),
                pl.BlockSpec((1, total_stations), lambda at, ref: (0, 0)),
            ],
            out_specs=pl.BlockSpec((2 * beams, 2 * total_stations), lambda at, ref: (at, 0)),
        ),
        cost_estimate=pl.CostEstimate(
            flops=60 * beam_phase.size, transcendentals=0, bytes_accessed=12 * beam_phase.size
        ),
    )(
        jnp.stack([station_at.astype(jnp.int32), number]),
        beam_phase,
        station_delay.reshape(1, total_stations),
    )

    *formed, power = pl.pallas_call(
        functools.partial(middle_kernel, places, halves, rank, pols),
        out_shape=[block] * group + [jax.ShapeDtypeStruct((places * pols, beams), jnp.float32)],
        in_specs=[vmem] * (group + 1),
        out_specs=[vmem] * (group + 1),
        scratch_shapes=[
            pltpu.VMEM((pols, halves, 2 * total_stations, times), jnp.bfloat16),
            pltpu.VMEM((places * pols, beams, 128), jnp.float32),
        ],
        cost_estimate=pl.CostEstimate(
            flops=8 * beams * places * total_stations * pols * halves * times,
            transcendentals=0,
            bytes_accessed=4 * group * rows * times,
        ),
    )(*held, weights)
    back = [formed[0]] + [swap_with(formed[o], o) for o in range(1, group)]

    power = power.reshape(places, pols, beams)
    bit = 1
    while bit < places:
        paired = power.reshape(power.shape[0] // 2, 2, pols, beams)
        power = paired[:, 0] + swap_with(paired[:, 1], bit)
        bit *= 2
    power = power.reshape(pols, beams)
    while bit < group:
        power = power + swap_with(power, bit)
        bit *= 2
    slices = lax.axis_size("channel")
    bit = 1
    while bit < slices:
        pairs = [(at, at ^ bit) for at in range(slices)]
        power = power + lax.ppermute(power, "channel", pairs)
        bit *= 2

    terms = float(chan_count * slices * times * halves)
    beam_output, subspace = pl.pallas_call(
        functools.partial(finish_kernel, terms),
        out_shape=[
            jax.ShapeDtypeStruct((2, chan_count, pols * beams, times), jnp.bfloat16),
            jax.ShapeDtypeStruct((2, chan_count, rank * pols, stations), jnp.float32),
        ],
        in_specs=[smem] + [vmem] * (group + 1),
        out_specs=[hbm, vmem],
        scratch_shapes=[
            pltpu.VMEM((group, 2, pols * beams, times), jnp.bfloat16),
            pltpu.SemaphoreType.DMA((group, 2)),
        ],
        cost_estimate=pl.CostEstimate(
            flops=0, transcendentals=0, bytes_accessed=4 * group * rows * times
        ),
    )(me_array, power, *back)
    return (
        beam_output.reshape(2, chan_count, pols, beams, times),
        subspace.reshape(2, chan_count, rank, pols, stations),
    )


def power_of_two(number):
    return number & (number - 1) == 0


def body(voltages, start_seed, beam_phase, station_delay):
    parts, chan_count, pols, stations, times = voltages.shape
    places, halves, slices = (lax.axis_size(axis) for axis in ("station", "tm", "channel"))
    fits = (
        chan_count == places * halves
        and all(power_of_two(size) for size in (places, halves, slices))
        and pols == 2
        and stations == 128
        and times == pols * stations
        and start_seed.shape[2] == 4
        and beam_phase.shape[0] == places * stations
    )
    return (fast_body if fits else general_body)(voltages, start_seed, beam_phase, station_delay)


def solution(mesh):
    in_specs = (
        P(None, "channel", None, "station", "tm"),
        P(None, "channel", None, None, "station"),
        P(),
        P(),
    )
    out_specs = (
        P(None, "channel", None, "station", "tm"),
        P(None, "channel", None, None, "station"),
    )
    return jax.shard_map(body, mesh=mesh, in_specs=in_specs, out_specs=out_specs, check_vma=False)
```

```python
import functools

import jax
import jax.numpy as jnp
from jax import lax
from jax.experimental import pallas as pl
from jax.experimental.pallas import tpu as pltpu
from jax.sharding import PartitionSpec as P


ITERS = 3
PHASES = 1024
GROUP = ("tm", "station")


HIGH = lax.Precision.HIGHEST
VMEM = pltpu.MemorySpace.VMEM
SMEM = pltpu.MemorySpace.SMEM
HBM = pltpu.MemorySpace.HBM


def coefficients(subspace, voltage):
    real_v = voltage[0].astype(jnp.float32)
    imag_v = voltage[1].astype(jnp.float32)
    pattern = "...kpm,...pmt->...kt"
    real_sum = jnp.einsum(pattern, subspace[0], real_v, precision=HIGH) + jnp.einsum(
        pattern, subspace[1], imag_v, precision=HIGH
    )
    imag_sum = jnp.einsum(pattern, subspace[0], imag_v, precision=HIGH) - jnp.einsum(
        pattern, subspace[1], real_v, precision=HIGH
    )
    return jnp.stack([real_sum, imag_sum])


def applied(voltage, coefficient):
    real_v = voltage[0].astype(jnp.float32)
    imag_v = voltage[1].astype(jnp.float32)
    pattern = "...pmt,...kt->...kpm"
    real_sum = jnp.einsum(pattern, real_v, coefficient[0], precision=HIGH) + jnp.einsum(
        pattern, imag_v, coefficient[1], precision=HIGH
    )
    imag_sum = jnp.einsum(pattern, imag_v, coefficient[0], precision=HIGH) - jnp.einsum(
        pattern, real_v, coefficient[1], precision=HIGH
    )
    return jnp.stack([real_sum, imag_sum])


def gram_matrix(image_field):
    pattern = "...kpm,...lpm->...kl"
    real_sum = jnp.einsum(pattern, image_field[0], image_field[0], precision=HIGH) + jnp.einsum(
        pattern, image_field[1], image_field[1], precision=HIGH
    )
    imag_sum = jnp.einsum(pattern, image_field[0], image_field[1], precision=HIGH) - jnp.einsum(
        pattern, image_field[1], image_field[0], precision=HIGH
    )
    return jnp.stack([real_sum, imag_sum])


def inverse_factor(gram_real, gram_imag):
    rank_count = gram_real.shape[-1]
    nothing = jnp.zeros_like(gram_real[..., 0, 0])
    low_real = {}
    low_imag = {}
    for column in range(rank_count):
        diagonal = gram_real[..., column, column]
        for middle in range(column):
            diagonal = diagonal - low_real[column, middle] ** 2 - low_imag[column, middle] ** 2
        pivot_root = jnp.sqrt(diagonal)
        low_real[column, column] = pivot_root
        low_imag[column, column] = nothing
        for row_at in range(column + 1, rank_count):
            acc_real = gram_real[..., row_at, column]
            acc_imag = gram_imag[..., row_at, column]
            for middle in range(column):
                acc_real = acc_real - (
                    low_real[row_at, middle] * low_real[column, middle]
                    + low_imag[row_at, middle] * low_imag[column, middle]
                )
                acc_imag = acc_imag - (
                    low_imag[row_at, middle] * low_real[column, middle]
                    - low_real[row_at, middle] * low_imag[column, middle]
                )
            low_real[row_at, column] = acc_real / pivot_root
            low_imag[row_at, column] = acc_imag / pivot_root
    inv_real = {}
    inv_imag = {}
    for column in range(rank_count):
        inv_real[column, column] = 1.0 / low_real[column, column]
        inv_imag[column, column] = nothing
        for row_at in range(column + 1, rank_count):
            acc_real = nothing
            acc_imag = nothing
            for middle in range(column, row_at):
                acc_real = (
                    acc_real
                    + low_real[row_at, middle] * inv_real[middle, column]
                    - low_imag[row_at, middle] * inv_imag[middle, column]
                )
                acc_imag = (
                    acc_imag
                    + low_real[row_at, middle] * inv_imag[middle, column]
                    + low_imag[row_at, middle] * inv_real[middle, column]
                )
            inv_real[row_at, column] = -acc_real / low_real[row_at, row_at]
            inv_imag[row_at, column] = -acc_imag / low_real[row_at, row_at]
    span = range(rank_count)
    real_rows = [jnp.stack([inv_real.get((r, c), nothing) for c in span], axis=-1) for r in span]
    imag_rows = [jnp.stack([inv_imag.get((r, c), nothing) for c in span], axis=-1) for r in span]
    return (jnp.stack(real_rows, axis=-2), jnp.stack(imag_rows, axis=-2))


def orthonormal(image_field, sums):
    inv_real, inv_imag = inverse_factor(sums[0], sums[1])
    pattern = "...lpm,...kl->...kpm"
    real_sum = jnp.einsum(pattern, image_field[0], inv_real, precision=HIGH) + jnp.einsum(
        pattern, image_field[1], inv_imag, precision=HIGH
    )
    imag_sum = jnp.einsum(pattern, image_field[1], inv_real, precision=HIGH) - jnp.einsum(
        pattern, image_field[0], inv_imag, precision=HIGH
    )
    return jnp.stack([real_sum, imag_sum])


def project_out(voltage, subspace, coefficient):
    pattern = "...kpm,...kt->...pmt"
    real_sum = jnp.einsum(pattern, subspace[0], coefficient[0], precision=HIGH) - jnp.einsum(
        pattern, subspace[1], coefficient[1], precision=HIGH
    )
    imag_sum = jnp.einsum(pattern, subspace[0], coefficient[1], precision=HIGH) + jnp.einsum(
        pattern, subspace[1], coefficient[0], precision=HIGH
    )
    return jnp.stack(
        [voltage[0].astype(jnp.float32) - real_sum, voltage[1].astype(jnp.float32) - imag_sum]
    )


def beam_weights(phase_rows, delays, channel_numbers):
    summed = phase_rows + delays[None, :]
    index = summed[None, :, :] * (channel_numbers[:, None, None] + 1) % PHASES
    angle = index.astype(jnp.float32) * (2.0 * jnp.pi / PHASES)
    norming = 1.0 / jnp.sqrt(jnp.float32(delays.shape[0]))
    return (
        (jnp.cos(angle) * norming).astype(jnp.bfloat16),
        (-jnp.sin(angle) * norming).astype(jnp.bfloat16),
    )


def form_beams(real_w, imag_w, cleaned):
    dot = functools.partial(jnp.einsum, "cbm,cpmt->cpbt", preferred_element_type=jnp.float32)
    real_sum = dot(real_w, cleaned[0]) - dot(imag_w, cleaned[1])
    imag_sum = dot(real_w, cleaned[1]) + dot(imag_w, cleaned[0])
    return jnp.stack([real_sum, imag_sum])


def general_body(voltages, start_seed, beam_phase, station_delay):
    chan_count = voltages.shape[1]
    first_channel = lax.axis_index("channel") * chan_count
    channel_numbers = jnp.arange(chan_count, dtype=jnp.int32) + first_channel
    subspace = start_seed.astype(jnp.float32)
    for _ in range(ITERS):
        coefficient = lax.psum(
            coefficients(subspace, voltages).astype(jnp.bfloat16), "station"
        ).astype(jnp.float32)
        summed = lax.psum(applied(voltages, coefficient), "tm")
        sums = lax.psum(gram_matrix(summed), "station")
        subspace = orthonormal(summed, sums)
    coefficient = lax.psum(coefficients(subspace, voltages).astype(jnp.bfloat16), "station").astype(
        jnp.float32
    )
    cleaned = project_out(voltages, subspace, coefficient).astype(jnp.bfloat16)
    beam_count = beam_phase.shape[0] // lax.axis_size("station")
    first_beam = lax.axis_index("station") * beam_count
    phase_rows = lax.dynamic_slice_in_dim(beam_phase, first_beam, beam_count, 0)
    real_w, imag_w = beam_weights(phase_rows, station_delay, channel_numbers)
    beam_field = form_beams(real_w, imag_w, lax.all_gather(cleaned, "station", axis=3, tiled=True))
    power_part = jnp.sum(beam_field[0] ** 2 + beam_field[1] ** 2, axis=(0, 3))
    terms = chan_count * lax.axis_size("channel") * voltages.shape[4] * lax.axis_size("tm")
    beam_power = lax.psum(power_part, ("tm", "channel")) / terms
    rescale = lax.rsqrt(beam_power + 1e-06)
    beam_output = (beam_field * rescale[None, None, :, :, None]).astype(jnp.bfloat16)
    return (beam_output, subspace)


def room(mebibytes):
    return pltpu.CompilerParams(vmem_limit_bytes=mebibytes * 2**20)


def pack_kernel(me_ref, volt_ref, seed_ref, *refs):
    group = len(refs) - 3
    outs, (held_ref, sem, seed_sem) = refs[:group], refs[group:]
    me = me_ref[0]
    rows = volt_ref.shape[2]
    seeds = pltpu.make_async_copy(seed_ref, held_ref, seed_sem)
    seeds.start()
    copies = []
    for place in range(group):
        for part in range(2):
            copy = pltpu.make_async_copy(
                volt_ref.at[part, me ^ place],
                outs[place].at[pl.ds(part * rows, rows)],
                sem.at[place, part],
            )
            copy.start()
            copies.append(copy)
    rank = seed_ref.shape[2] // 2
    seeds.wait()
    for place in range(group):
        halves = []
        for part in range(2):
            pols = [
                held_ref[part, me ^ place, pl.ds(pol, rank, stride=2), :] for pol in range(2)
            ]
            halves.append(jnp.concatenate(pols, axis=1))
        start = jnp.concatenate(halves, axis=0).astype(jnp.float32)
        outs[place][2 * rows :, :] = start.astype(jnp.bfloat16)
    for copy in copies:
        copy.wait()


def cos_sin(index):
    quarter = PHASES // 4
    turn = (index + quarter // 2) // quarter if quarter & (quarter - 1) else (
        (index + quarter // 2) >> (quarter.bit_length() - 1)
    )
    rest = index - turn * quarter
    angle = rest.astype(jnp.float32) * (2.0 * jnp.pi / PHASES)
    square = angle * angle
    cos = 1.0 + square * (
        -0.5 + square * (1.0 / 24 + square * (-1.0 / 720 + square * (1.0 / 40320)))
    )
    sin = angle * (
        1.0 + square * (-1.0 / 6 + square * (1.0 / 120 + square * (-1.0 / 5040 + square * (1.0 / 362880))))
    )
    odd = (turn & 1) == 1
    base_cos = jnp.where(odd, sin, cos)
    base_sin = jnp.where(odd, cos, sin)
    flip_cos = ((turn + 1) & 2) == 2
    flip_sin = (turn & 2) == 2
    return jnp.where(flip_cos, -base_cos, base_cos), jnp.where(flip_sin, -base_sin, base_sin)


def weight_kernel(stations, scalars_ref, phase_ref, delay_ref, out_ref):
    mine, number = scalars_ref[0], scalars_ref[1]
    beams = phase_ref.shape[0]
    wide = stations
    places = phase_ref.shape[1] // wide
    norming = 1.0 / jnp.sqrt(jnp.float32(phase_ref.shape[1]))
    for place in range(places):
        column = pl.multiple_of((mine ^ place) * wide, wide)
        summed = phase_ref[:, pl.ds(column, wide)] + delay_ref[:, pl.ds(column, wide)]
        cos, sin = cos_sin((summed * number) & (PHASES - 1))
        real = (cos * norming).astype(jnp.bfloat16)
        imag = (-sin * norming).astype(jnp.bfloat16)
        first = pl.ds(place * wide, wide)
        second = pl.ds((places + place) * wide, wide)
        out_ref[:beams, first] = real
        out_ref[:beams, second] = -imag
        out_ref[beams:, first] = imag
        out_ref[beams:, second] = real


def split(value, count):
    parts = []
    for _ in range(count - 1):
        part = value.astype(jnp.bfloat16)
        parts.append(part)
        value = value - part.astype(jnp.float32)
    return parts + [value.astype(jnp.bfloat16)]


def nn(a, b):
    return lax.dot_general(a, b, (((1,), (0,)), ((), ())), preferred_element_type=jnp.float32)


def nt(a, b):
    return lax.dot_general(a, b, (((1,), (1,)), ((), ())), preferred_element_type=jnp.float32)


def tn(a, b):
    return lax.dot_general(a, b, (((0,), (0,)), ((), ())), preferred_element_type=jnp.float32)


def first_kernel(places, halves, rank, *refs):
    group = places * halves
    x, weight_ref, y = refs[:group], refs[group], refs[group + 1 : group + 1 + places]
    state_ref, rows_ref, sum_ref, clean_ref = refs[group + 1 + places :]
    inputs = (x[0].shape[0] - 2 * rank) // 2
    times = x[0].shape[1]
    rows = 2 * rank
    row_at = lax.broadcasted_iota(jnp.int32, (rows, 1), 0)
    top = row_at < rank
    sign = jnp.where(top, 1.0, -1.0).astype(jnp.float32)
    row_mod = jnp.where(top, row_at, row_at - rank)

    def swap(value):
        return jnp.concatenate([value[rank:], value[:rank]], axis=0)

    def fold(value):
        total = value[:rows]
        for piece in range(1, value.shape[0] // rows):
            total = total + value[piece * rows : (piece + 1) * rows]
        return total

    def coefficient_of(field, count):
        left = []
        for value in field:
            both = jnp.concatenate([sign * value, swap(value)], axis=1)
            left.append(jnp.concatenate(split(both, count), axis=0))
        out = []
        for half in range(halves):
            total = None
            for place in range(places):
                term = nn(left[place], x[half * places + place][: 2 * inputs, :])
                total = term if total is None else total + term
            out.append(fold(total))
        return out

    def image_of(coefficient):
        left = [jnp.concatenate(split(value, 3), axis=0) for value in coefficient]
        out = []
        for place in range(places):
            total = None
            for half in range(halves):
                term = nt(left[half], x[half * places + place][: 2 * inputs, :])
                total = term if total is None else total + term
            total = fold(total)
            out.append(swap(total[:, inputs:]) + sign * total[:, :inputs])
        return out

    def whitener(field):
        column = []
        for line in range(rows):
            total = None
            for value in field:
                term = jnp.sum(value * value[line : line + 1], axis=1, keepdims=True)
                total = term if total is None else total + term
            column.append(total)
        real, imag = [], []
        for line in range(rank):
            value = column[line] + swap(column[line + rank])
            real.append(jnp.where(top, value, swap(value)))
            value = column[line + rank] - swap(column[line])
            imag.append(jnp.where(top, value, swap(value)))
        zero = jnp.zeros((rows, 1), jnp.float32)
        inv_real = [jnp.where(row_mod == line, 1.0, zero) for line in range(rank)]
        inv_imag = [zero] * rank
        pivots = zero
        for step in range(rank):
            pivot = real[step][step : step + 1]
            pivots = jnp.where(row_mod == step, pivot, pivots)
            if step == rank - 1:
                break
            below = row_mod > step
            inverse = 1.0 / pivot
            mul_real = jnp.where(below, real[step] * inverse, 0.0)
            mul_imag = jnp.where(below, imag[step] * inverse, 0.0)

            def reduce(re, im):
                at_re, at_im = re[step : step + 1], im[step : step + 1]
                return (
                    re - (mul_real * at_re - mul_imag * at_im),
                    im - (mul_real * at_im + mul_imag * at_re),
                )

            for line in range(step + 1, rank):
                real[line], imag[line] = reduce(real[line], imag[line])
            for line in range(step + 1):
                inv_real[line], inv_imag[line] = reduce(inv_real[line], inv_imag[line])
        scale = 1.0 / jnp.sqrt(pivots)
        return [value * scale for value in inv_real], [value * scale for value in inv_imag]

    def basis(field, white):
        real, imag = white
        out = []
        for value in field:
            total = jnp.zeros_like(value)
            for line in range(rank):
                total = total + jnp.where(top, real[line], -imag[line]) * value[line : line + 1]
                total = total + jnp.where(top, imag[line], real[line]) * value[line + rank : line + rank + 1]
            out.append(total)
        return out

    def whitened(raw, white):
        real, imag = white
        out = []
        for value in raw:
            total = jnp.zeros_like(value)
            for line in range(rank):
                total = total + jnp.where(top, real[line], imag[line]) * value[line : line + 1]
                total = total + jnp.where(top, -imag[line], real[line]) * value[line + rank : line + rank + 1]
            out.append(total)
        return out

    start = [x[place][2 * inputs : 2 * inputs + rows, :].astype(jnp.float32) for place in range(places)]
    coefficient = coefficient_of(start, 1)
    for _ in range(ITERS):
        field = image_of(coefficient)
        raw = coefficient_of(field, 3)
        white = whitener(field)
        coefficient = whitened(raw, white)
    subspace = basis(field, white)

    for place in range(places):
        state_ref[:, place * inputs : (place + 1) * inputs] = subspace[place]
    for half in range(1, halves):
        first = places * inputs + (half - 1) * times
        state_ref[:, first : first + times] = coefficient[half]
    for place in range(places):
        rows_ref[place] = jnp.concatenate(split(subspace[place], 2), axis=0)
    form_half(x[:places], subspace, coefficient[0], weight_ref, clean_ref, y, rows_ref, sum_ref, True)


def form_half(x, subspace, coefficient, weight_ref, clean_ref, y, rows_ref, sum_ref, fresh):
    places, (rows, inputs), times = len(x), subspace[0].shape, coefficient.shape[1]
    rank = rows // 2
    pols = clean_ref.shape[0]
    wide = inputs // pols
    top = lax.broadcasted_iota(jnp.int32, (rows, 1), 0) < rank
    sign = jnp.where(top, 1.0, -1.0).astype(jnp.float32)
    turned = jnp.concatenate([coefficient[rank:], coefficient[:rank]], axis=0)
    high, low = split(jnp.concatenate([sign * coefficient, turned], axis=1), 2)
    right = jnp.concatenate([high, high, low], axis=0)
    for place in range(places):
        high, low = split(subspace[place], 2)
        gone = tn(jnp.concatenate([high, low, high], axis=0), right)
        for part in range(2):
            for pol in range(pols):
                at = part * inputs + pol * wide
                value = x[place][at : at + wide, :].astype(jnp.float32)
                value = value - gone[pol * wide : (pol + 1) * wide, part * times : (part + 1) * times]
                first = (part * places + place) * wide
                clean_ref[pol, first : first + wide, :] = value.astype(jnp.bfloat16)
    beams = weight_ref.shape[0] // (2 * places)
    for place in range(places):
        y[place][2 * inputs :, :] = rows_ref[place]
        for pol in range(pols):
            out = nn(weight_ref[2 * place * beams : 2 * (place + 1) * beams, :], clean_ref[pol])
            for part in range(2):
                at = part * inputs + pol * beams
                y[place][at : at + beams, :] = out[part * beams : (part + 1) * beams].astype(
                    jnp.bfloat16
                )
            square = out * out
            square = square[:beams] + square[beams:]
            lanes = square[:, :128]
            for lane in range(128, times, 128):
                lanes = lanes + square[:, lane : lane + 128]
            if fresh:
                sum_ref[place * pols + pol] = lanes
            else:
                sum_ref[place * pols + pol] += lanes


def second_kernel(places, *refs):
    x, (weight_ref, state_ref, rows_ref, before_ref) = refs[:places], refs[places : places + 4]
    y, (power_ref, clean_ref, sum_ref) = refs[places + 4 : 2 * places + 4], refs[2 * places + 4 :]
    inputs = clean_ref.shape[0] * clean_ref.shape[1] // (2 * places)
    subspace = [state_ref[:, place * inputs : (place + 1) * inputs] for place in range(places)]
    coefficient = state_ref[:, places * inputs :]
    sum_ref[...] = before_ref[...]
    form_half(x, subspace, coefficient, weight_ref, clean_ref, y, rows_ref, sum_ref, False)
    for line in range(sum_ref.shape[0]):
        power_ref[line : line + 1, :] = jnp.sum(sum_ref[line].T, axis=0, keepdims=True)


def finish_kernel(terms, me_ref, power_ref, *refs):
    *y, out_ref, base_ref, held, sem = refs
    me = me_ref[0]
    pols = power_ref.shape[0]
    beams = power_ref.shape[1]
    rescale = lax.rsqrt(power_ref[...] * (1.0 / terms) + 1e-06)
    square = jnp.concatenate([rescale, jnp.zeros((beams - pols, beams), jnp.float32)], axis=0).T
    scale = [jnp.broadcast_to(square[:, pol : pol + 1], (beams, y[0].shape[1])) for pol in range(pols)]
    inputs = pols * beams
    copies = []
    for place, source in enumerate(y):
        for part in range(2):
            for pol in range(pols):
                at = part * inputs + pol * beams
                value = source[at : at + beams, :].astype(jnp.float32) * scale[pol]
                held[place, part, pol * beams : (pol + 1) * beams, :] = value.astype(jnp.bfloat16)
            copy = pltpu.make_async_copy(
                held.at[place, part], out_ref.at[part, me ^ place], sem.at[place, part]
            )
            copy.start()
            copies.append(copy)
    rows = (y[0].shape[0] - 2 * inputs) // 2
    rank = rows // 2
    for place, source in enumerate(y):
        both = source[2 * inputs :, :].astype(jnp.float32)
        value = both[:rows] + both[rows:]
        for part in range(2):
            for pol in range(pols):
                base_ref[part, me ^ place, pl.ds(pol, rank, stride=pols), :] = value[
                    part * rank : (part + 1) * rank, pol * beams : (pol + 1) * beams
                ]
    for copy in copies:
        copy.wait()


def fast_body(voltages, start_seed, beam_phase, station_delay):
    _, chan_count, pols, stations, times = voltages.shape
    rank = start_seed.shape[2]
    places, halves = lax.axis_size("station"), lax.axis_size("tm")
    group = places * halves
    inputs = pols * stations
    station_at, tm_at = lax.axis_index("station"), lax.axis_index("tm")
    me = (tm_at * places + station_at).astype(jnp.int32)
    number = (lax.axis_index("channel") * chan_count + me + 1).astype(jnp.int32)
    me_array = me.reshape(1)
    rows = 2 * inputs + 4 * rank
    block = pltpu.VMEM((rows, times), jnp.bfloat16)
    raw_block = pltpu.VMEM((2 * inputs + 2 * rank, times), jnp.bfloat16)
    vmem = pl.BlockSpec(memory_space=VMEM)
    smem = pl.BlockSpec(memory_space=SMEM)
    hbm = pl.BlockSpec(memory_space=HBM)

    def swap_with(value, offset):
        pairs = [(at, at ^ offset) for at in range(group)]
        return lax.ppermute(value, GROUP, pairs)

    packed = pl.pallas_call(
        pack_kernel,
        out_shape=[raw_block] * group,
        in_specs=[smem, hbm, hbm],
        out_specs=[vmem] * group,
        scratch_shapes=[
            pltpu.VMEM((2, chan_count, rank * pols, stations), jnp.int32),
            pltpu.SemaphoreType.DMA((group, 2)),
            pltpu.SemaphoreType.DMA,
        ],
        compiler_params=room(6),
        cost_estimate=pl.CostEstimate(
            flops=0, transcendentals=0, bytes_accessed=4 * group * rows * times
        ),
    )(
        me_array,
        pltpu.with_memory_space_constraint(voltages.reshape(2, chan_count, inputs, times), HBM),
        pltpu.with_memory_space_constraint(
            start_seed.reshape(2, chan_count, rank * pols, stations), HBM
        ),
    )
    held = [packed[0]] + [swap_with(packed[o], o) for o in range(1, group)]

    total_stations = places * stations
    beams = beam_phase.shape[0] // places
    weights = pl.pallas_call(
        functools.partial(weight_kernel, stations),
        out_shape=jax.ShapeDtypeStruct((2 * places * beams, 2 * total_stations), jnp.bfloat16),
        grid_spec=pltpu.PrefetchScalarGridSpec(
            num_scalar_prefetch=1,
            grid=(places,),
            in_specs=[
                pl.BlockSpec((beams, total_stations), lambda at, ref: (ref[0] ^ at, 0)),
                pl.BlockSpec((1, total_stations), lambda at, ref: (0, 0)),
            ],
            out_specs=pl.BlockSpec((2 * beams, 2 * total_stations), lambda at, ref: (at, 0)),
        ),
        compiler_params=room(8),
        cost_estimate=pl.CostEstimate(
            flops=60 * beam_phase.size, transcendentals=0, bytes_accessed=12 * beam_phase.size
        ),
    )(
        jnp.stack([station_at.astype(jnp.int32), number]),
        pltpu.with_memory_space_constraint(beam_phase, HBM),
        pltpu.with_memory_space_constraint(station_delay.reshape(1, total_stations), HBM),
    )

    lines = places * pols
    lane_sums = pltpu.VMEM((lines, beams, 128), jnp.float32)
    clean = pltpu.VMEM((pols, 2 * total_stations, times), jnp.bfloat16)
    basis_rows = pltpu.VMEM((places, 4 * rank, times), jnp.bfloat16)
    work = 8 * beams * places * total_stations * pols * times
    *early, state, basis_rows_of, sums = pl.pallas_call(
        functools.partial(first_kernel, places, halves, rank),
        out_shape=[block] * places
        + [
            pltpu.VMEM((2 * rank, places * inputs + (halves - 1) * times), jnp.float32),
            basis_rows,
            lane_sums,
        ],
        in_specs=[vmem] * (group + 1),
        out_specs=[vmem] * (places + 3),
        scratch_shapes=[clean],
        compiler_params=room(16),
        cost_estimate=pl.CostEstimate(
            flops=2 * work, transcendentals=0, bytes_accessed=3 * group * rows * times
        ),
    )(*held, weights)
    back = [early[0]] + [swap_with(early[o], o) for o in range(1, places)]
    *late, power = pl.pallas_call(
        functools.partial(second_kernel, places),
        out_shape=[block] * places + [jax.ShapeDtypeStruct((lines, beams), jnp.float32)],
        in_specs=[vmem] * (places + 4),
        out_specs=[vmem] * (places + 1),
        scratch_shapes=[clean, lane_sums],
        compiler_params=room(12),
        cost_estimate=pl.CostEstimate(
            flops=work, transcendentals=0, bytes_accessed=2 * group * rows * times
        ),
    )(*held[places:], weights, state, basis_rows_of, sums)

    power = power.reshape(places, pols, beams)
    power = power + swap_with(power, places)
    power = functools.reduce(
        jnp.add,
        [power[0]] + [swap_with(power[o], o) for o in range(1, places)],
    )
    back += [swap_with(late[o], places + o) for o in range(places)]
    slices = lax.axis_size("channel")
    bit = 1
    while bit < slices:
        pairs = [(at, at ^ bit) for at in range(slices)]
        power = power + lax.ppermute(power, "channel", pairs)
        bit *= 2

    terms = float(chan_count * slices * times * halves)
    beam_output, subspace = pl.pallas_call(
        functools.partial(finish_kernel, terms),
        out_shape=[
            jax.ShapeDtypeStruct((2, chan_count, pols * beams, times), jnp.bfloat16),
            jax.ShapeDtypeStruct((2, chan_count, rank * pols, stations), jnp.float32),
        ],
        in_specs=[smem] + [vmem] * (group + 1),
        out_specs=[hbm, vmem],
        scratch_shapes=[
            pltpu.VMEM((group, 2, pols * beams, times), jnp.bfloat16),
            pltpu.SemaphoreType.DMA((group, 2)),
        ],
        compiler_params=room(10),
        cost_estimate=pl.CostEstimate(
            flops=0, transcendentals=0, bytes_accessed=4 * group * rows * times
        ),
    )(me_array, power, *back)
    return (
        beam_output.reshape(2, chan_count, pols, beams, times),
        subspace.reshape(2, chan_count, rank, pols, stations),
    )


def power_of_two(number):
    return number & (number - 1) == 0


def body(voltages, start_seed, beam_phase, station_delay):
    _, chan_count, pols, stations, times = voltages.shape
    places, halves, slices = (lax.axis_size(axis) for axis in ("station", "tm", "channel"))
    fits = (
        chan_count == places * halves
        and all(power_of_two(size) for size in (places, halves, slices))
        and halves == 2
        and pols == 2
        and stations == 128
        and times == pols * stations
        and start_seed.shape[2] == 4
        and beam_phase.shape[0] == places * stations
    )
    return (fast_body if fits else general_body)(voltages, start_seed, beam_phase, station_delay)


def solution(mesh):
    in_specs = (
        P(None, "channel", None, "station", "tm"),
        P(None, "channel", None, None, "station"),
        P(),
        P(),
    )
    out_specs = (
        P(None, "channel", None, "station", "tm"),
        P(None, "channel", None, None, "station"),
    )
    return jax.shard_map(body, mesh=mesh, in_specs=in_specs, out_specs=out_specs, check_vma=False)
```

```python
import functools

import jax
import jax.numpy as jnp
from jax import lax
from jax.experimental import pallas as pl
from jax.experimental.pallas import tpu as pltpu
from jax.sharding import PartitionSpec as P


ITERS = 3
PHASES = 1024
GROUP = ("tm", "station")
EARLY = (0, 1, 2, 3, 4)


HIGH = lax.Precision.HIGHEST
VMEM = pltpu.MemorySpace.VMEM
SMEM = pltpu.MemorySpace.SMEM
HBM = pltpu.MemorySpace.HBM


def coefficients(subspace, voltage):
    real_v = voltage[0].astype(jnp.float32)
    imag_v = voltage[1].astype(jnp.float32)
    pattern = "...kpm,...pmt->...kt"
    real_sum = jnp.einsum(pattern, subspace[0], real_v, precision=HIGH) + jnp.einsum(
        pattern, subspace[1], imag_v, precision=HIGH
    )
    imag_sum = jnp.einsum(pattern, subspace[0], imag_v, precision=HIGH) - jnp.einsum(
        pattern, subspace[1], real_v, precision=HIGH
    )
    return jnp.stack([real_sum, imag_sum])


def applied(voltage, coefficient):
    real_v = voltage[0].astype(jnp.float32)
    imag_v = voltage[1].astype(jnp.float32)
    pattern = "...pmt,...kt->...kpm"
    real_sum = jnp.einsum(pattern, real_v, coefficient[0], precision=HIGH) + jnp.einsum(
        pattern, imag_v, coefficient[1], precision=HIGH
    )
    imag_sum = jnp.einsum(pattern, imag_v, coefficient[0], precision=HIGH) - jnp.einsum(
        pattern, real_v, coefficient[1], precision=HIGH
    )
    return jnp.stack([real_sum, imag_sum])


def gram_matrix(image_field):
    pattern = "...kpm,...lpm->...kl"
    real_sum = jnp.einsum(pattern, image_field[0], image_field[0], precision=HIGH) + jnp.einsum(
        pattern, image_field[1], image_field[1], precision=HIGH
    )
    imag_sum = jnp.einsum(pattern, image_field[0], image_field[1], precision=HIGH) - jnp.einsum(
        pattern, image_field[1], image_field[0], precision=HIGH
    )
    return jnp.stack([real_sum, imag_sum])


def inverse_factor(gram_real, gram_imag):
    rank_count = gram_real.shape[-1]
    nothing = jnp.zeros_like(gram_real[..., 0, 0])
    low_real = {}
    low_imag = {}
    for column in range(rank_count):
        diagonal = gram_real[..., column, column]
        for middle in range(column):
            diagonal = diagonal - low_real[column, middle] ** 2 - low_imag[column, middle] ** 2
        pivot_root = jnp.sqrt(diagonal)
        low_real[column, column] = pivot_root
        low_imag[column, column] = nothing
        for row_at in range(column + 1, rank_count):
            acc_real = gram_real[..., row_at, column]
            acc_imag = gram_imag[..., row_at, column]
            for middle in range(column):
                acc_real = acc_real - (
                    low_real[row_at, middle] * low_real[column, middle]
                    + low_imag[row_at, middle] * low_imag[column, middle]
                )
                acc_imag = acc_imag - (
                    low_imag[row_at, middle] * low_real[column, middle]
                    - low_real[row_at, middle] * low_imag[column, middle]
                )
            low_real[row_at, column] = acc_real / pivot_root
            low_imag[row_at, column] = acc_imag / pivot_root
    inv_real = {}
    inv_imag = {}
    for column in range(rank_count):
        inv_real[column, column] = 1.0 / low_real[column, column]
        inv_imag[column, column] = nothing
        for row_at in range(column + 1, rank_count):
            acc_real = nothing
            acc_imag = nothing
            for middle in range(column, row_at):
                acc_real = (
                    acc_real
                    + low_real[row_at, middle] * inv_real[middle, column]
                    - low_imag[row_at, middle] * inv_imag[middle, column]
                )
                acc_imag = (
                    acc_imag
                    + low_real[row_at, middle] * inv_imag[middle, column]
                    + low_imag[row_at, middle] * inv_real[middle, column]
                )
            inv_real[row_at, column] = -acc_real / low_real[row_at, row_at]
            inv_imag[row_at, column] = -acc_imag / low_real[row_at, row_at]
    span = range(rank_count)
    real_rows = [jnp.stack([inv_real.get((r, c), nothing) for c in span], axis=-1) for r in span]
    imag_rows = [jnp.stack([inv_imag.get((r, c), nothing) for c in span], axis=-1) for r in span]
    return (jnp.stack(real_rows, axis=-2), jnp.stack(imag_rows, axis=-2))


def orthonormal(image_field, sums):
    inv_real, inv_imag = inverse_factor(sums[0], sums[1])
    pattern = "...lpm,...kl->...kpm"
    real_sum = jnp.einsum(pattern, image_field[0], inv_real, precision=HIGH) + jnp.einsum(
        pattern, image_field[1], inv_imag, precision=HIGH
    )
    imag_sum = jnp.einsum(pattern, image_field[1], inv_real, precision=HIGH) - jnp.einsum(
        pattern, image_field[0], inv_imag, precision=HIGH
    )
    return jnp.stack([real_sum, imag_sum])


def project_out(voltage, subspace, coefficient):
    pattern = "...kpm,...kt->...pmt"
    real_sum = jnp.einsum(pattern, subspace[0], coefficient[0], precision=HIGH) - jnp.einsum(
        pattern, subspace[1], coefficient[1], precision=HIGH
    )
    imag_sum = jnp.einsum(pattern, subspace[0], coefficient[1], precision=HIGH) + jnp.einsum(
        pattern, subspace[1], coefficient[0], precision=HIGH
    )
    return jnp.stack(
        [voltage[0].astype(jnp.float32) - real_sum, voltage[1].astype(jnp.float32) - imag_sum]
    )


def beam_weights(phase_rows, delays, channel_numbers):
    summed = phase_rows + delays[None, :]
    index = summed[None, :, :] * (channel_numbers[:, None, None] + 1) % PHASES
    angle = index.astype(jnp.float32) * (2.0 * jnp.pi / PHASES)
    norming = 1.0 / jnp.sqrt(jnp.float32(delays.shape[0]))
    return (
        (jnp.cos(angle) * norming).astype(jnp.bfloat16),
        (-jnp.sin(angle) * norming).astype(jnp.bfloat16),
    )


def form_beams(real_w, imag_w, cleaned):
    dot = functools.partial(jnp.einsum, "cbm,cpmt->cpbt", preferred_element_type=jnp.float32)
    real_sum = dot(real_w, cleaned[0]) - dot(imag_w, cleaned[1])
    imag_sum = dot(real_w, cleaned[1]) + dot(imag_w, cleaned[0])
    return jnp.stack([real_sum, imag_sum])


def general_body(voltages, start_seed, beam_phase, station_delay):
    chan_count = voltages.shape[1]
    first_channel = lax.axis_index("channel") * chan_count
    channel_numbers = jnp.arange(chan_count, dtype=jnp.int32) + first_channel
    subspace = start_seed.astype(jnp.float32)
    for _ in range(ITERS):
        coefficient = lax.psum(
            coefficients(subspace, voltages).astype(jnp.bfloat16), "station"
        ).astype(jnp.float32)
        summed = lax.psum(applied(voltages, coefficient), "tm")
        sums = lax.psum(gram_matrix(summed), "station")
        subspace = orthonormal(summed, sums)
    coefficient = lax.psum(coefficients(subspace, voltages).astype(jnp.bfloat16), "station").astype(
        jnp.float32
    )
    cleaned = project_out(voltages, subspace, coefficient).astype(jnp.bfloat16)
    beam_count = beam_phase.shape[0] // lax.axis_size("station")
    first_beam = lax.axis_index("station") * beam_count
    phase_rows = lax.dynamic_slice_in_dim(beam_phase, first_beam, beam_count, 0)
    real_w, imag_w = beam_weights(phase_rows, station_delay, channel_numbers)
    beam_field = form_beams(real_w, imag_w, lax.all_gather(cleaned, "station", axis=3, tiled=True))
    power_part = jnp.sum(beam_field[0] ** 2 + beam_field[1] ** 2, axis=(0, 3))
    terms = chan_count * lax.axis_size("channel") * voltages.shape[4] * lax.axis_size("tm")
    beam_power = lax.psum(power_part, ("tm", "channel")) / terms
    rescale = lax.rsqrt(beam_power + 1e-06)
    beam_output = (beam_field * rescale[None, None, :, :, None]).astype(jnp.bfloat16)
    return (beam_output, subspace)


def room(mebibytes):
    return pltpu.CompilerParams(vmem_limit_bytes=mebibytes * 2**20)


def pack_kernel(which, me_ref, volt_ref, seed_ref, *refs):
    outs, (held_ref, sem, seed_sem) = refs[: len(which)], refs[len(which) :]
    me = me_ref[0]
    rows = volt_ref.shape[2]
    copies = []
    for line, place in enumerate(which):
        channel = me ^ place
        copies.append(
            pltpu.make_async_copy(seed_ref.at[:, channel], held_ref.at[line], seed_sem.at[line])
        )
    for line, place in enumerate(which):
        for part in range(2):
            copies.append(
                pltpu.make_async_copy(
                    volt_ref.at[part, me ^ place],
                    outs[line].at[pl.ds(part * rows, rows)],
                    sem.at[line, part],
                )
            )
    for copy in copies:
        copy.start()
    rank = seed_ref.shape[2] // 2
    for line in range(len(which)):
        copies[line].wait()
        halves = []
        for part in range(2):
            pols = [held_ref[line, part, pl.ds(pol, rank, stride=2), :] for pol in range(2)]
            halves.append(jnp.concatenate(pols, axis=1))
        start = jnp.concatenate(halves, axis=0).astype(jnp.float32)
        outs[line][2 * rows :, :] = start.astype(jnp.bfloat16)
    for copy in copies[len(which) :]:
        copy.wait()


def cos_sin(index):
    quarter = PHASES // 4
    turn = (index + quarter // 2) // quarter if quarter & (quarter - 1) else (
        (index + quarter // 2) >> (quarter.bit_length() - 1)
    )
    rest = index - turn * quarter
    angle = rest.astype(jnp.float32) * (2.0 * jnp.pi / PHASES)
    square = angle * angle
    cos = 1.0 + square * (
        -0.5 + square * (1.0 / 24 + square * (-1.0 / 720 + square * (1.0 / 40320)))
    )
    sin = angle * (
        1.0 + square * (-1.0 / 6 + square * (1.0 / 120 + square * (-1.0 / 5040 + square * (1.0 / 362880))))
    )
    odd = (turn & 1) == 1
    base_cos = jnp.where(odd, sin, cos)
    base_sin = jnp.where(odd, cos, sin)
    flip_cos = ((turn + 1) & 2) == 2
    flip_sin = (turn & 2) == 2
    return jnp.where(flip_cos, -base_cos, base_cos), jnp.where(flip_sin, -base_sin, base_sin)


def weight_kernel(stations, scalars_ref, phase_ref, delay_ref, out_ref):
    mine, number = scalars_ref[0], scalars_ref[1]
    beams = phase_ref.shape[0]
    wide = stations
    places = phase_ref.shape[1] // wide
    norming = 1.0 / jnp.sqrt(jnp.float32(phase_ref.shape[1]))
    for place in range(places):
        column = pl.multiple_of((mine ^ place) * wide, wide)
        summed = phase_ref[:, pl.ds(column, wide)] + delay_ref[:, pl.ds(column, wide)]
        cos, sin = cos_sin((summed * number) & (PHASES - 1))
        real = (cos * norming).astype(jnp.bfloat16)
        imag = (-sin * norming).astype(jnp.bfloat16)
        first = pl.ds(place * wide, wide)
        second = pl.ds((places + place) * wide, wide)
        out_ref[:beams, first] = real
        out_ref[:beams, second] = -imag
        out_ref[beams:, first] = imag
        out_ref[beams:, second] = real


def split(value, count):
    parts = []
    for _ in range(count - 1):
        part = value.astype(jnp.bfloat16)
        parts.append(part)
        value = value - part.astype(jnp.float32)
    return parts + [value.astype(jnp.bfloat16)]


def nn(a, b):
    return lax.dot_general(a, b, (((1,), (0,)), ((), ())), preferred_element_type=jnp.float32)


def nt(a, b):
    return lax.dot_general(a, b, (((1,), (1,)), ((), ())), preferred_element_type=jnp.float32)


def tn(a, b):
    return lax.dot_general(a, b, (((0,), (0,)), ((), ())), preferred_element_type=jnp.float32)


def first_kernel(places, halves, rank, *refs):
    group = places * halves
    x, weight_ref, y = refs[:group], refs[group], refs[group + 1 : group + 1 + places]
    state_ref, rows_ref, sum_ref, clean_ref = refs[group + 1 + places :]
    inputs = (x[0].shape[0] - 2 * rank) // 2
    times = x[0].shape[1]
    rows = 2 * rank
    row_at = lax.broadcasted_iota(jnp.int32, (rows, 1), 0)
    top = row_at < rank
    sign = jnp.where(top, 1.0, -1.0).astype(jnp.float32)
    row_mod = jnp.where(top, row_at, row_at - rank)

    def swap(value):
        return jnp.concatenate([value[rank:], value[:rank]], axis=0)

    def fold(value):
        total = value[:rows]
        for piece in range(1, value.shape[0] // rows):
            total = total + value[piece * rows : (piece + 1) * rows]
        return total

    def coefficient_of(field, count):
        left = []
        for value in field:
            both = jnp.concatenate([sign * value, swap(value)], axis=1)
            left.append(jnp.concatenate(split(both, count), axis=0))
        out = []
        for half in range(halves):
            total = None
            for place in range(places):
                term = nn(left[place], x[half * places + place][: 2 * inputs, :])
                total = term if total is None else total + term
            out.append(fold(total))
        return out

    def image_of(coefficient):
        left = [jnp.concatenate(split(value, 3), axis=0) for value in coefficient]
        out = []
        for place in range(places):
            total = None
            for half in range(halves):
                term = nt(left[half], x[half * places + place][: 2 * inputs, :])
                total = term if total is None else total + term
            total = fold(total)
            out.append(swap(total[:, inputs:]) + sign * total[:, :inputs])
        return out

    def whitener(field):
        column = []
        for line in range(rows):
            total = None
            for value in field:
                term = jnp.sum(value * value[line : line + 1], axis=1, keepdims=True)
                total = term if total is None else total + term
            column.append(total)
        real, imag = [], []
        for line in range(rank):
            value = column[line] + swap(column[line + rank])
            real.append(jnp.where(top, value, swap(value)))
            value = column[line + rank] - swap(column[line])
            imag.append(jnp.where(top, value, swap(value)))
        zero = jnp.zeros((rows, 1), jnp.float32)
        inv_real = [jnp.where(row_mod == line, 1.0, zero) for line in range(rank)]
        inv_imag = [zero] * rank
        pivots = zero
        for step in range(rank):
            pivot = real[step][step : step + 1]
            pivots = jnp.where(row_mod == step, pivot, pivots)
            if step == rank - 1:
                break
            below = row_mod > step
            inverse = 1.0 / pivot
            mul_real = jnp.where(below, real[step] * inverse, 0.0)
            mul_imag = jnp.where(below, imag[step] * inverse, 0.0)

            def reduce(re, im):
                at_re, at_im = re[step : step + 1], im[step : step + 1]
                return (
                    re - (mul_real * at_re - mul_imag * at_im),
                    im - (mul_real * at_im + mul_imag * at_re),
                )

            for line in range(step + 1, rank):
                real[line], imag[line] = reduce(real[line], imag[line])
            for line in range(step + 1):
                inv_real[line], inv_imag[line] = reduce(inv_real[line], inv_imag[line])
        scale = 1.0 / jnp.sqrt(pivots)
        return [value * scale for value in inv_real], [value * scale for value in inv_imag]

    def basis(field, white):
        real, imag = white
        out = []
        for value in field:
            total = jnp.zeros_like(value)
            for line in range(rank):
                total = total + jnp.where(top, real[line], -imag[line]) * value[line : line + 1]
                total = total + jnp.where(top, imag[line], real[line]) * value[line + rank : line + rank + 1]
            out.append(total)
        return out

    def whitened(raw, white):
        real, imag = white
        out = []
        for value in raw:
            total = jnp.zeros_like(value)
            for line in range(rank):
                total = total + jnp.where(top, real[line], imag[line]) * value[line : line + 1]
                total = total + jnp.where(top, -imag[line], real[line]) * value[line + rank : line + rank + 1]
            out.append(total)
        return out

    start = [x[place][2 * inputs : 2 * inputs + rows, :].astype(jnp.float32) for place in range(places)]
    coefficient = coefficient_of(start, 1)
    for _ in range(ITERS):
        field = image_of(coefficient)
        raw = coefficient_of(field, 3)
        white = whitener(field)
        coefficient = whitened(raw, white)
    subspace = basis(field, white)

    for place in range(places):
        state_ref[:, place * inputs : (place + 1) * inputs] = subspace[place]
    for half in range(1, halves):
        first = places * inputs + (half - 1) * times
        state_ref[:, first : first + times] = coefficient[half]
    for place in range(places):
        rows_ref[place] = jnp.concatenate(split(subspace[place], 2), axis=0)
    form_half(x[:places], subspace, coefficient[0], weight_ref, clean_ref, y, rows_ref, sum_ref, True)


def form_half(x, subspace, coefficient, weight_ref, clean_ref, y, rows_ref, sum_ref, fresh):
    places, (rows, inputs), times = len(x), subspace[0].shape, coefficient.shape[1]
    rank = rows // 2
    pols = clean_ref.shape[0]
    wide = inputs // pols
    top = lax.broadcasted_iota(jnp.int32, (rows, 1), 0) < rank
    sign = jnp.where(top, 1.0, -1.0).astype(jnp.float32)
    turned = jnp.concatenate([coefficient[rank:], coefficient[:rank]], axis=0)
    high, low = split(jnp.concatenate([sign * coefficient, turned], axis=1), 2)
    right = jnp.concatenate([high, high, low], axis=0)
    for place in range(places):
        high, low = split(subspace[place], 2)
        gone = tn(jnp.concatenate([high, low, high], axis=0), right)
        for part in range(2):
            for pol in range(pols):
                at = part * inputs + pol * wide
                value = x[place][at : at + wide, :].astype(jnp.float32)
                value = value - gone[pol * wide : (pol + 1) * wide, part * times : (part + 1) * times]
                first = (part * places + place) * wide
                clean_ref[pol, first : first + wide, :] = value.astype(jnp.bfloat16)
    beams = weight_ref.shape[0] // (2 * places)
    for place in range(places):
        y[place][2 * inputs :, :] = rows_ref[place]
        for pol in range(pols):
            out = nn(weight_ref[2 * place * beams : 2 * (place + 1) * beams, :], clean_ref[pol])
            for part in range(2):
                at = part * inputs + pol * beams
                y[place][at : at + beams, :] = out[part * beams : (part + 1) * beams].astype(
                    jnp.bfloat16
                )
            square = out * out
            square = square[:beams] + square[beams:]
            lanes = square[:, :128]
            for lane in range(128, times, 128):
                lanes = lanes + square[:, lane : lane + 128]
            if fresh:
                sum_ref[place * pols + pol] = lanes
            else:
                sum_ref[place * pols + pol] += lanes


def second_kernel(places, *refs):
    x, (weight_ref, state_ref, rows_ref, before_ref) = refs[:places], refs[places : places + 4]
    y, (power_ref, clean_ref, sum_ref) = refs[places + 4 : 2 * places + 4], refs[2 * places + 4 :]
    inputs = clean_ref.shape[0] * clean_ref.shape[1] // (2 * places)
    subspace = [state_ref[:, place * inputs : (place + 1) * inputs] for place in range(places)]
    coefficient = state_ref[:, places * inputs :]
    sum_ref[...] = before_ref[...]
    form_half(x, subspace, coefficient, weight_ref, clean_ref, y, rows_ref, sum_ref, False)
    for line in range(sum_ref.shape[0]):
        power_ref[line : line + 1, :] = jnp.sum(sum_ref[line].T, axis=0, keepdims=True)


def finish_kernel(terms, which, me_ref, power_ref, *refs):
    y = refs[: len(which)]
    out_ref, base_ref, held, kept, sem = refs[-5:]
    me = me_ref[0]
    pols, beams = power_ref.shape
    rescale = lax.rsqrt(power_ref[...] * (1.0 / terms) + 1e-06)
    square = jnp.concatenate([rescale, jnp.zeros((beams - pols, beams), jnp.float32)], axis=0).T
    scale = [jnp.broadcast_to(square[:, pol : pol + 1], (beams, y[0].shape[1])) for pol in range(pols)]
    inputs = pols * beams
    rows = (y[0].shape[0] - 2 * inputs) // 2
    rank = rows // 2
    copies = []
    for line, place in enumerate(which):
        source = y[line]
        both = source[2 * inputs :, :].astype(jnp.float32)
        value = both[:rows] + both[rows:]
        for part in range(2):
            for pol in range(pols):
                at = part * inputs + pol * beams
                scaled = source[at : at + beams, :].astype(jnp.float32) * scale[pol]
                held[line, part, pol * beams : (pol + 1) * beams, :] = scaled.astype(jnp.bfloat16)
                kept[line, part, pl.ds(pol, rank, stride=pols), :] = value[
                    part * rank : (part + 1) * rank, pol * beams : (pol + 1) * beams
                ]
            copies.append(
                pltpu.make_async_copy(
                    held.at[line, part], out_ref.at[part, me ^ place], sem.at[line, part, 0]
                )
            )
            copies[-1].start()
            copies.append(
                pltpu.make_async_copy(
                    kept.at[line, part], base_ref.at[part, me ^ place], sem.at[line, part, 1]
                )
            )
            copies[-1].start()
    for copy in copies:
        copy.wait()


def fast_body(voltages, start_seed, beam_phase, station_delay):
    _, chan_count, pols, stations, times = voltages.shape
    rank = start_seed.shape[2]
    places, halves = lax.axis_size("station"), lax.axis_size("tm")
    group = places * halves
    inputs = pols * stations
    station_at, tm_at = lax.axis_index("station"), lax.axis_index("tm")
    me = (tm_at * places + station_at).astype(jnp.int32)
    number = (lax.axis_index("channel") * chan_count + me + 1).astype(jnp.int32)
    me_array = me.reshape(1)
    rows = 2 * inputs + 4 * rank
    block = pltpu.VMEM((rows, times), jnp.bfloat16)
    raw_block = pltpu.VMEM((2 * inputs + 2 * rank, times), jnp.bfloat16)
    vmem = pl.BlockSpec(memory_space=VMEM)
    smem = pl.BlockSpec(memory_space=SMEM)
    hbm = pl.BlockSpec(memory_space=HBM)

    def swap_with(value, offset):
        pairs = [(at, at ^ offset) for at in range(group)]
        return lax.ppermute(value, GROUP, pairs)

    volt_blocks = pltpu.with_memory_space_constraint(
        voltages.reshape(2, chan_count, inputs, times), HBM
    )
    seed_blocks = pltpu.with_memory_space_constraint(
        start_seed.reshape(2, chan_count, rank * pols, stations), HBM
    )

    def pack(which):
        return pl.pallas_call(
            functools.partial(pack_kernel, which),
            out_shape=[raw_block] * len(which),
            in_specs=[smem, hbm, hbm],
            out_specs=[vmem] * len(which),
            scratch_shapes=[
                pltpu.VMEM((len(which), 2, rank * pols, stations), jnp.int32),
                pltpu.SemaphoreType.DMA((len(which), 2)),
                pltpu.SemaphoreType.DMA((len(which),)),
            ],
            compiler_params=room(4),
            cost_estimate=pl.CostEstimate(
                flops=0, transcendentals=0, bytes_accessed=4 * len(which) * rows * times
            ),
        )(me_array, volt_blocks, seed_blocks)

    first_places = tuple(range(1, places))
    other_places = tuple(range(places, group)) + (0,)
    packed = dict(zip(first_places, pack(first_places)))
    packed.update(zip(other_places, pack(other_places)))
    held = [packed[0]] + [swap_with(packed[o], o) for o in range(1, group)]

    total_stations = places * stations
    beams = beam_phase.shape[0] // places
    weights = pl.pallas_call(
        functools.partial(weight_kernel, stations),
        out_shape=jax.ShapeDtypeStruct((2 * places * beams, 2 * total_stations), jnp.bfloat16),
        grid_spec=pltpu.PrefetchScalarGridSpec(
            num_scalar_prefetch=1,
            grid=(places,),
            in_specs=[
                pl.BlockSpec((beams, total_stations), lambda at, ref: (ref[0] ^ at, 0)),
                pl.BlockSpec((1, total_stations), lambda at, ref: (0, 0)),
            ],
            out_specs=pl.BlockSpec((2 * beams, 2 * total_stations), lambda at, ref: (at, 0)),
        ),
        compiler_params=room(8),
        cost_estimate=pl.CostEstimate(
            flops=60 * beam_phase.size, transcendentals=0, bytes_accessed=12 * beam_phase.size
        ),
    )(
        jnp.stack([station_at.astype(jnp.int32), number]),
        pltpu.with_memory_space_constraint(beam_phase, HBM),
        pltpu.with_memory_space_constraint(station_delay.reshape(1, total_stations), HBM),
    )

    lines = places * pols
    lane_sums = pltpu.VMEM((lines, beams, 128), jnp.float32)
    clean = pltpu.VMEM((pols, 2 * total_stations, times), jnp.bfloat16)
    basis_rows = pltpu.VMEM((places, 4 * rank, times), jnp.bfloat16)
    work = 8 * beams * places * total_stations * pols * times
    *early, state, basis_rows_of, sums = pl.pallas_call(
        functools.partial(first_kernel, places, halves, rank),
        out_shape=[block] * places
        + [
            pltpu.VMEM((2 * rank, places * inputs + (halves - 1) * times), jnp.float32),
            basis_rows,
            lane_sums,
        ],
        in_specs=[vmem] * (group + 1),
        out_specs=[vmem] * (places + 3),
        scratch_shapes=[clean],
        compiler_params=room(16),
        cost_estimate=pl.CostEstimate(
            flops=2 * work, transcendentals=0, bytes_accessed=3 * group * rows * times
        ),
    )(*held, weights)
    back = [early[0]] + [swap_with(early[o], o) for o in range(1, places)]
    *late, power = pl.pallas_call(
        functools.partial(second_kernel, places),
        out_shape=[block] * places + [jax.ShapeDtypeStruct((lines, beams), jnp.float32)],
        in_specs=[vmem] * (places + 4),
        out_specs=[vmem] * (places + 1),
        scratch_shapes=[clean, lane_sums],
        compiler_params=room(12),
        cost_estimate=pl.CostEstimate(
            flops=work, transcendentals=0, bytes_accessed=2 * group * rows * times
        ),
    )(*held[places:], weights, state, basis_rows_of, sums)

    power = power.reshape(places, pols, beams)
    power = power + swap_with(power, places)
    power = functools.reduce(
        jnp.add,
        [power[0]] + [swap_with(power[o], o) for o in range(1, places)],
    )
    back += [swap_with(late[o], places + o) for o in range(places)]
    slices = lax.axis_size("channel")
    own = power
    for offset in range(1, slices):
        pairs = [(at, at ^ offset) for at in range(slices)]
        power = power + lax.ppermute(own, "channel", pairs)

    terms = float(chan_count * slices * times * halves)
    outputs = []
    for which in (EARLY, tuple(o for o in range(group) if o not in EARLY)):
        outputs = pl.pallas_call(
            functools.partial(finish_kernel, terms, which),
            out_shape=[
                jax.ShapeDtypeStruct((2, chan_count, pols * beams, times), jnp.bfloat16),
                jax.ShapeDtypeStruct((2, chan_count, rank * pols, stations), jnp.float32),
            ],
            in_specs=[smem] + [vmem] * (len(which) + 1) + [hbm] * len(outputs),
            out_specs=[hbm, hbm],
            scratch_shapes=[
                pltpu.VMEM((len(which), 2, pols * beams, times), jnp.bfloat16),
                pltpu.VMEM((len(which), 2, rank * pols, stations), jnp.float32),
                pltpu.SemaphoreType.DMA((len(which), 2, 2)),
            ],
            input_output_aliases={len(which) + 2 + at: at for at in range(len(outputs))},
            compiler_params=room(8),
            cost_estimate=pl.CostEstimate(
                flops=0, transcendentals=0, bytes_accessed=4 * len(which) * rows * times
            ),
        )(me_array, power, *(back[o] for o in which), *outputs)
    beam_output, subspace = outputs
    return (
        beam_output.reshape(2, chan_count, pols, beams, times),
        subspace.reshape(2, chan_count, rank, pols, stations),
    )


def power_of_two(number):
    return number & (number - 1) == 0


def body(voltages, start_seed, beam_phase, station_delay):
    _, chan_count, pols, stations, times = voltages.shape
    places, halves, slices = (lax.axis_size(axis) for axis in ("station", "tm", "channel"))
    fits = (
        chan_count == places * halves
        and all(power_of_two(size) for size in (places, halves, slices))
        and halves == 2
        and pols == 2
        and stations == 128
        and times == pols * stations
        and start_seed.shape[2] == 4
        and beam_phase.shape[0] == places * stations
    )
    return (fast_body if fits else general_body)(voltages, start_seed, beam_phase, station_delay)


def solution(mesh):
    in_specs = (
        P(None, "channel", None, "station", "tm"),
        P(None, "channel", None, None, "station"),
        P(),
        P(),
    )
    out_specs = (
        P(None, "channel", None, "station", "tm"),
        P(None, "channel", None, None, "station"),
    )
    return jax.shard_map(body, mesh=mesh, in_specs=in_specs, out_specs=out_specs, check_vma=False)
```
